512 devices in a mesh: doc: 128 (over z_lo, y, x, core), filt: 4 (over z_hi).
Axes of the slice: x: 4, y: 8, z: 8 (z_hi: 4, z_lo: 2; z = z_hi * 2 + z_lo), core: 2. Of those that a mesh axis runs over, the one named last changes fastest.
Arguments:
- embedded: bfloat16 [256, 256, 256], P('doc'), may hold values from -8 to 8
- lengths: int32 [256], P('doc'), may hold values from 1 to 256, 26214 in all
- conv_weight: bfloat16 [256, 15, 1024], P(None, None, 'filt'), may hold values from -0.15625 to 0.15625
- head_weight: bfloat16 [3, 1024], P(None, 'filt'), may hold values from -0.109375 to 0.109375
- occupation: int32 [256], P('doc'), may hold values from 0 to 839
- cohort: int32 [256], P('doc'), may hold values from 0 to 39
- education: int32 [256], P('doc'), may hold values from 0 to 7
- occ_table: float32 [840], replicated, may hold values from -3 to 3
- cohort_table: float32 [40], replicated, may hold values from -3 to 3
- edu_table: float32 [8], replicated, may hold values from -3 to 3
- wage: float32 [256], P('doc'), may hold values from -8 to 8
Outputs:
- conv_grad: float32 [256, 15, 1024], P('doc', None, 'filt')
- head_grad: float32 [3, 1024], P(None, 'filt')
- occ_grad: float32 [840], replicated
- cohort_grad: float32 [40], replicated
- edu_grad: float32 [8], replicated
- prediction: float32 [256], P('doc')
The draws below stay inside these ranges and needn't reach their ends.
All inputs are finite; a program needn't handle non-finite values. No bound on the sum of `lengths` on one device may be relied on, other than what follows from the above.
Results may differ from the reference program's by a relative error of at most 0.0029.
Values sent between devices are 32-bit elements; how exact they have to be, the bound alone decides.
A program may use at most 64 MiB of HBM per device.

```python
import math
import jax
import jax.numpy as jnp
import numpy as np
from jax import lax

E = 256
F = 1024
TAPS = 15
OCC = 840
COH = 40
EDU = 8
SEQ = 256
POSTS = 256


def draw_embedded(key, part):
    first_key, second_key = jax.random.split(key)
    scale = jnp.exp(jax.random.uniform(first_key, (POSTS, 1, 1), jnp.float32, math.log(0.5), math.log(2.0)))
    values = jnp.clip(jax.random.normal(second_key, (POSTS, SEQ, E), jnp.float32), -4.0, 4.0) * scale
    return values.astype(jnp.bfloat16)


def set_ends(array, own_key, smallest, largest):
    index_at = [jax.random.randint(jax.random.fold_in(own_key, axis), (), 0, length) for axis, length in enumerate(array.shape)]
    widest = array.shape.index(max(array.shape))
    next_to = index_at[:widest] + [(index_at[widest] + 1) % array.shape[widest]] + index_at[widest + 1:]
    return array.at[tuple(index_at)].set(smallest).at[tuple(next_to)].set(largest)


def level_of(stream_key, shape, shards, least, largest):
    gain = 1.0
    for dim, blocks in shards:
        heights = jax.random.uniform(jax.random.fold_in(jax.random.fold_in(stream_key, 6), dim), (blocks,), jnp.float32, least / len(shards), largest / len(shards))
        gain = gain * jnp.repeat(jnp.exp(heights), shape[dim] // blocks).reshape((-1,) + (1,) * (len(shape) - 1 - dim))
    return gain


def rank_table(number_of, skew):
    loads = [(1 << 20) // math.isqrt(grade ** skew) + 1 for grade in range(1, number_of + 1)]
    scale = 1 + sum(loads) // (1 << 30)
    return np.cumsum(np.array([max(1, weight // scale) for weight in loads]))


def ranked_ids(stream_key, shape, number_of, lean):
    listing = rank_table(number_of, lean)
    ticket = jax.random.randint(jax.random.fold_in(stream_key, 1), shape, 0, int(listing[number_of - 1]))
    grade = jnp.searchsorted(jnp.asarray(listing, jnp.int32), ticket, side="right")
    return jax.random.permutation(jax.random.fold_in(stream_key, 2), number_of)[grade].astype(jnp.int32)


def split_up(count, total, most, skew):
    loads = [(1 << 20) // math.isqrt(grade ** skew) + 1 for grade in range(2, count + 1)]
    surplus, counts = total - most - (count - 1), [1] * (count - 1)
    while surplus > 0:
        free = [i for i in range(count - 1) if counts[i] < most]
        mass, left = sum([loads[i] for i in free]), surplus
        for i in free:
            addition = min(most - counts[i], max(1, left * loads[i] // mass), surplus)
            counts[i] = counts[i] + addition
            surplus = surplus - addition
    return np.array([most] + counts)


def uneven(key, amount, total, reach, lean):
    if amount == 2:
        one = jax.random.randint(key, (), max(1, total - reach), min(reach, total - 1) + 1)
        return jnp.stack([one, total - one])
    tallies = jnp.asarray(split_up(amount, total, reach, lean), jnp.int32)
    pairs = (amount - 1) // 2
    giver, sink = tallies[1:1 + 2 * pairs:2], tallies[2:2 + 2 * pairs:2]
    margin = jnp.minimum(giver - 1, reach - sink)
    passed = jax.random.randint(jax.random.fold_in(key, 1), (pairs,), 0, 1 << 20) % (margin + 1)
    tallies = tallies.at[1:1 + 2 * pairs:2].set(giver - passed).at[2:2 + 2 * pairs:2].set(sink + passed)
    return tallies[jax.random.permutation(jax.random.fold_in(key, 2), amount)]


def centred(key, extent, width, most, cuts=(), held_as=jnp.bfloat16):
    factor_of = level_of(key, extent, cuts, -0.22, 0.18) if cuts else 1.0
    entries = jax.random.normal(key, extent, jnp.float32) * width * factor_of
    return jnp.minimum(jnp.maximum(entries, -most), most).astype(held_as)


def setup_inputs(seed: int = 0) -> dict:
    splits = jax.random.split(jax.random.key(seed), 12)
    return {
        "embedded": draw_embedded(jax.random.fold_in(splits[11], 71), 0),
        "lengths": uneven(splits[1], POSTS, POSTS * SEQ * 2 // 5, SEQ, 2).astype(jnp.int32),
        "conv_weight": centred(splits[2], (E, TAPS, F), (E * 5) ** -0.5, 0.15625, ((2, 4),)),
        "head_weight": centred(splits[3], (3, F), (3 * F) ** -0.5, 0.109375, ((1, 4),)),
        "occupation": set_ends(ranked_ids(splits[4], (POSTS,), OCC, 2), jax.random.fold_in(splits[4], 3), 0, OCC - 1).astype(jnp.int32),
        "cohort": set_ends(jax.random.randint(splits[5], (POSTS,), 0, COH), jax.random.fold_in(splits[5], 1), 0, COH - 1).astype(jnp.int32),
        "education": set_ends(jax.random.randint(splits[6], (POSTS,), 0, EDU), jax.random.fold_in(splits[6], 1), 0, EDU - 1).astype(jnp.int32),
        "occ_table": centred(splits[7], (OCC,), 0.5, 3.0, (), jnp.float32),
        "cohort_table": centred(splits[8], (COH,), 0.5, 3.0, (), jnp.float32),
        "edu_table": centred(splits[9], (EDU,), 0.5, 3.0, (), jnp.float32),
        "wage": centred(splits[10], (POSTS,), 2.0, 8.0, ((0, 128),), jnp.float32),
    }


TAU = 0.05
WIDTH_LIST = ((3, 0), (5, 3), (7, 8))


def reference(embedded, lengths, conv_weight, head_weight, occupation, cohort, education, occ_table, cohort_table, edu_table, wage):
    positions = jnp.arange(SEQ, dtype=jnp.int32)
    head = head_weight.astype(jnp.float32)
    offsets = occ_table[occupation] + cohort_table[cohort] + edu_table[education]
    matrices = []
    for taps, first in WIDTH_LIST:
        matrices.append(jnp.transpose(conv_weight[:, first:first + taps, :], (1, 0, 2)).reshape(taps * E, F))

    def one_post(carry, item):
        tokens, length, extra, goal = item
        valid = positions < length
        masked = jnp.where(valid[:, None], tokens, jnp.zeros_like(tokens))
        padded = jnp.pad(masked, ((3, 3), (0, 0)))
        columns = jnp.stack([padded[offset:offset + SEQ] for offset in range(7)], axis=1)
        features = []
        shares = []
        pieces = []
        for index in range(3):
            taps = WIDTH_LIST[index][0]
            half = (taps - 1) // 2
            window = columns[:, 3 - half:3 + half + 1, :].reshape(SEQ, taps * E)
            conv = jnp.dot(window, matrices[index], preferred_element_type=jnp.float32)
            score = jnp.where(valid[:, None], conv / TAU, -jnp.inf)
            top = jnp.max(score, axis=0)
            expd = jnp.exp(score - top[None, :])
            total = jnp.sum(expd, axis=0)
            features.append(TAU * (top + jnp.log(total)))
            shares.append(expd / total[None, :])
            pieces.append(window)
        feature = jnp.stack(features)
        pred = jnp.sum(feature * head) + extra
        resid = pred - goal
        grads = []
        for index in range(3):
            taps = WIDTH_LIST[index][0]
            slope = (resid * head[index][None, :] * shares[index]).astype(jnp.bfloat16)
            term = jnp.dot(pieces[index].T, slope, preferred_element_type=jnp.float32)
            grads.append(jnp.transpose(term.reshape(taps, E, F), (1, 0, 2)))
        conv_total = carry[0] + jnp.concatenate(grads, axis=1)
        head_total = carry[1] + resid * feature
        return (conv_total, head_total), (pred, resid)

    start = (jnp.zeros((E, TAPS, F), jnp.float32), jnp.zeros((3, F), jnp.float32))
    (conv_grad, head_grad), (prediction, residual) = lax.scan(one_post, start, (embedded, lengths, offsets, wage))
    occ_grad = jax.ops.segment_sum(residual, occupation, OCC)
    cohort_grad = jax.ops.segment_sum(residual, cohort, COH)
    edu_grad = jax.ops.segment_sum(residual, education, EDU)
    return conv_grad, head_grad, occ_grad, cohort_grad, edu_grad, prediction
```

```python
import jax
import jax.numpy as jnp
from jax import lax
from jax.experimental import pallas as pl
from jax.experimental.pallas import tpu as pltpu
from jax.sharding import PartitionSpec as P

TAU = 0.05
WIDTH_LIST = ((3, 0), (5, 3), (7, 8))
NZ, NY, NX = 2, 8, 4
HALF_ROWS = 4096
KEEP = 2048
F32 = jnp.float32


def convolve(columns, weights):
    outputs = []
    for taps, first in WIDTH_LIST:
        half = (taps - 1) // 2
        window = columns[:, :, 3 - half : 3 + half + 1, :]
        outputs.append(
            jnp.einsum(
                "ptje,ejf->ptf",
                window,
                weights[:, first : first + taps, :],
                preferred_element_type=jnp.float32,
            )
        )
    return tuple(outputs)


def kernel(
    occ_ref, coh_ref, edu_ref, rows_ref, feat_ref, head_ref, cols_ref, share_ref,
    conv_out, small_out, pred_out,
    pred_buf, slope, grad, from_core, kept, from_y, from_xa, from_xb, from_yb, from_z,
    sums, sum_core, sum_z, sum_x, sum_y,
    pred_send, pred_recv, core_send, core_recv, chain_send, chain_recv,
    xa_send, xa_recv, xb_send, xb_recv, yb_send, yb_recv, z_send, z_recv,
    s_send, s_recv, sx_send, sx_recv, sy_send, sy_recv,
):
    doc = lax.axis_index("doc")
    filt = lax.axis_index("filt")
    c = lax.rem(doc, 2)
    x = lax.rem(doc // 2, NX)
    y = lax.rem(doc // (2 * NX), NY)
    z = doc // (2 * NX * NY)

    def at(z_to, y_to, x_to, c_to):
        return {"doc": ((z_to * NY + y_to) * NX + x_to) * 2 + c_to}

    def x_plus(d):
        return lax.rem(x + d, NX)

    def y_plus(d):
        return lax.rem(y + d, NY)

    core_to = at(z, y, x, 1 - c)
    z_to = at(1 - z, y, x, c)
    x_to = [at(z, y, x_plus(d), c) for d in range(1, NX)]
    y_to = [at(z, y_plus(d), x, c) for d in range(1, NY)]
    filt_to = [{"filt": lax.rem(filt + d, 4)} for d in range(1, 4)]

    barrier = pltpu.get_barrier_semaphore()
    partners = [core_to, z_to] + x_to + y_to + filt_to
    for to in partners:
        pl.semaphore_signal(barrier, inc=1, device_id=to, device_id_type=pl.DeviceIdType.MESH)
    pl.semaphore_wait(barrier, len(partners))

    started = []

    def send(src, dst, send_sem, recv_sem, to):
        copy = pltpu.make_async_remote_copy(
            src_ref=src, dst_ref=dst, send_sem=send_sem, recv_sem=recv_sem,
            device_id=to, device_id_type=pl.DeviceIdType.MESH,
        )
        copy.start()
        started.append(copy)
        return copy

    pred_copies = [
        send(rows_ref.at[0], pred_buf.at[filt], pred_send.at[d], pred_recv.at[d], filt_to[d])
        for d in range(3)
    ]
    pred_buf[filt] = rows_ref[0]
    for copy in pred_copies:
        copy.wait_recv()
    pred = pred_buf[0] + pred_buf[1] + pred_buf[2] + pred_buf[3] + rows_ref[1]
    pred_out[...] = pred
    resid = pred - rows_ref[2]

    grid_row = lax.broadcasted_iota(jnp.int32, (8, 256), 0)
    grid_lane = lax.broadcasted_iota(jnp.int32, (8, 256), 1)
    small = jnp.zeros((8, 256), F32)
    for p in range(2):
        r = resid[p : p + 1, :]
        r = jnp.concatenate([r, r], axis=1)
        for w in range(3):
            scale = r * head_ref[w : w + 1, :].astype(F32)
            value = (scale * share_ref[w, p]).astype(jnp.bfloat16)
            for h in range(2):
                slope[h, p * 256 : (p + 1) * 256, w * 128 : (w + 1) * 128] = value[
                    :, h * 128 : (h + 1) * 128
                ]
        rb = jnp.broadcast_to(r, (8, 256))
        zero = jnp.zeros((8, 256), F32)
        small += rb * feat_ref[p]
        small += jnp.where((grid_row - 4) * 256 + grid_lane == occ_ref[p], rb, zero)
        small += jnp.where((grid_row == 3) & (grid_lane == coh_ref[p]), rb, zero)
        small += jnp.where((grid_row == 3) & (grid_lane - 128 == edu_ref[p]), rb, zero)
    sums[0] = small
    s_core = send(sums.at[0], sum_core, s_send.at[0], s_recv.at[0], core_to)

    core_copies = []
    for h in range(2):
        base = h * HALF_ROWS
        for k in range(7):
            low = max(0, abs(k - 3) - 1)
            part = lax.dot_general(
                cols_ref[k, :, h * 256 : (h + 1) * 256],
                slope[h, :, low * 128 :],
                (((0,), (0,)), ((), ())),
                preferred_element_type=F32,
            )
            for w in range(low, 3):
                taps, first = WIDTH_LIST[w]
                tap = first + k - 3 + (taps - 1) // 2
                grad[pl.ds(base + tap, 256, stride=16), :] = part[
                    :, (w - low) * 128 : (w - low + 1) * 128
                ]
        grad[pl.ds(base + 15, 256, stride=16), :] = jnp.zeros((256, 128), F32)
        core_copies.append(
            send(
                grad.at[pl.ds(base + (1 - c) * KEEP, KEEP)],
                from_core.at[h], core_send.at[h], core_recv.at[h], core_to,
            )
        )

    def take_core(h):
        core_copies[h].wait_recv()

        @pl.loop(0, KEEP // 256)
        def _(b):
            rows = pl.ds(b * 256, 256)
            mine = pl.ds(h * HALF_ROWS + c * KEEP + b * 256, 256)
            kept[h, rows, :] = grad[mine, :] + from_core[h, rows, :]

    counts = ((4, 3), (3, 4))
    chain = {}

    def chain_rows(u, owner):
        return pl.ds(owner * 256 + u * 128, 128)

    def chain_step(s):
        for u in range(2):
            for way in range(2):
                n = counts[u][way]
                if s >= n:
                    continue
                owner = y_plus(n - s) if way == 0 else y_plus(NY - n + s)
                rows = chain_rows(u, owner)
                if s > 0:
                    chain[u, way, s - 1].wait_recv()
                    kept[0, rows, :] = kept[0, rows, :] + from_y[u, way, s - 1]
                chain[u, way, s] = send(
                    kept.at[0, rows], from_y.at[u, way, s],
                    chain_send.at[u, way, s], chain_recv.at[u, way, s],
                    y_to[0] if way == 0 else y_to[NY - 2],
                )

    take_core(0)
    chain_step(0)
    take_core(1)
    xb = [
        send(
            kept.at[1, pl.ds(x_plus(d) * 512, 512)], from_xb.at[d - 1],
            xb_send.at[d - 1], xb_recv.at[d - 1], x_to[d - 1],
        )
        for d in range(1, NX)
    ]
    s_core.wait_recv()
    sums[1] = sums[0] + sum_core[...]
    s_z = send(sums.at[1], sum_z, s_send.at[1], s_recv.at[1], z_to)
    chain_step(1)
    s_z.wait_recv()
    sums[2] = sums[1] + sum_z[...]
    sum_x[x] = sums[2]
    sx = [
        send(sums.at[2], sum_x.at[x], sx_send.at[d - 1], sx_recv.at[d - 1], x_to[d - 1])
        for d in range(1, NX)
    ]
    chain_step(2)
    for copy in sx:
        copy.wait_recv()
    sums[3] = sum_x[0] + sum_x[1] + sum_x[2] + sum_x[3]
    sum_y[y] = sums[3]
    sy = [
        send(sums.at[3], sum_y.at[y], sy_send.at[d - 1], sy_recv.at[d - 1], y_to[d - 1])
        for d in range(1, NY)
    ]
    chain_step(3)

    for copy in xb:
        copy.wait_recv()
    mine_x = pl.ds(x * 512, 512)
    kept[1, mine_x, :] = kept[1, mine_x, :] + from_xb[0] + from_xb[1] + from_xb[2]
    yb = [
        send(
            kept.at[1, pl.ds(x * 512 + y_plus(d) * 64, 64)], from_yb.at[d - 1],
            yb_send.at[d - 1], yb_recv.at[d - 1], y_to[d - 1],
        )
        for d in range(1, NY)
    ]

    for u in range(2):
        rows = chain_rows(u, y)
        total = kept[0, rows, :]
        for way in range(2):
            last = counts[u][way] - 1
            chain[u, way, last].wait_recv()
            total += from_y[u, way, last]
        kept[0, rows, :] = total
    xa = [
        send(
            kept.at[0, pl.ds(y * 256 + x_plus(d) * 64, 64)], from_xa.at[d - 1],
            xa_send.at[d - 1], xa_recv.at[d - 1], x_to[d - 1],
        )
        for d in range(1, NX)
    ]

    for copy in xa:
        copy.wait_recv()
    row_a = y * 256 + x * 64
    rows = pl.ds(row_a, 64)
    kept[0, rows, :] = kept[0, rows, :] + from_xa[0] + from_xa[1] + from_xa[2]
    za = send(kept.at[0, pl.ds(row_a + (1 - z) * 32, 32)], from_z.at[0], z_send.at[0], z_recv.at[0], z_to)
    for copy in yb:
        copy.wait_recv()
    row_b = x * 512 + y * 64
    rows = pl.ds(row_b, 64)
    total = kept[1, rows, :]
    for d in range(NY - 1):
        total += from_yb[d]
    kept[1, rows, :] = total
    zb = send(kept.at[1, pl.ds(row_b + (1 - z) * 32, 32)], from_z.at[1], z_send.at[1], z_recv.at[1], z_to)
    for copy in sy:
        copy.wait_recv()
    total = sum_y[0]
    for d in range(1, NY):
        total += sum_y[d]
    small_out[...] = total
    for h, (copy, row) in enumerate(((za, row_a), (zb, row_b))):
        copy.wait_recv()
        value = kept[h, pl.ds(row + z * 32, 32), :] + from_z[h]
        for i in range(2):
            conv_out[i, :, h * 128 : (h + 1) * 128] = value[i * 16 : (i + 1) * 16, :]
    for copy in started:
        copy.wait_send()


def rows8(values):
    return jnp.pad(jnp.broadcast_to(values[:, None], (2, 128)), ((0, 6), (0, 0)))


def local(
    embedded,
    lengths,
    conv_weight,
    head_weight,
    occupation,
    cohort,
    education,
    occ_table,
    cohort_table,
    edu_table,
    wage,
):
    posts, seq_len, _ = embedded.shape
    positions = jnp.arange(seq_len, dtype=jnp.int32)
    valid = positions[None, :] < lengths[:, None]
    masked = jnp.where(valid[:, :, None], embedded, jnp.zeros_like(embedded))
    padded = jnp.pad(masked, ((0, 0), (3, 3), (0, 0)))
    columns = jnp.stack([padded[:, offset : offset + seq_len, :] for offset in range(7)], axis=2)
    convs = convolve(columns, conv_weight)
    features = []
    shares = []
    for conv in convs:
        score = jnp.where(valid[:, :, None], conv / TAU, -jnp.inf)
        top = jnp.max(score, axis=1, keepdims=True)
        expd = jnp.exp(score - top)
        total = jnp.sum(expd, axis=1, keepdims=True)
        features.append(TAU * (top[:, 0, :] + jnp.log(total[:, 0, :])))
        shares.append(expd / total)
    feature = jnp.stack(features, axis=1)
    head = head_weight.astype(jnp.float32)
    partial_pred = jnp.sum(feature * head[None, :, :], axis=(1, 2))
    occ_hot = (
        occupation[:, None] == jnp.arange(occ_table.shape[0], dtype=jnp.int32)[None, :]
    ).astype(jnp.float32)
    cohort_hot = (
        cohort[:, None] == jnp.arange(cohort_table.shape[0], dtype=jnp.int32)[None, :]
    ).astype(jnp.float32)
    edu_hot = (
        education[:, None] == jnp.arange(edu_table.shape[0], dtype=jnp.int32)[None, :]
    ).astype(jnp.float32)
    offsets = (
        jnp.sum(occ_hot * occ_table[None, :], axis=1)
        + jnp.sum(cohort_hot * cohort_table[None, :], axis=1)
        + jnp.sum(edu_hot * edu_table[None, :], axis=1)
    )

    e = jnp.arange(256, dtype=jnp.int32)[:, None]
    spot = jnp.arange(512, dtype=jnp.int32)[None, :]
    i, c, x, y, z = e % 2, (e // 2) % 2, (e // 4) % 4, (e // 16) % 8, e // 128
    place_a = c * 128 + y * 16 + x * 4 + z * 2 + i
    place_b = 256 + c * 128 + x * 32 + y * 4 + z * 2 + i
    picks = ((spot == place_a) | (spot == place_b)).astype(jnp.bfloat16)
    ordered = jnp.einsum(
        "pte,ek->ptk", masked, picks, preferred_element_type=jnp.float32
    ).astype(jnp.bfloat16)
    ordered = jnp.pad(ordered, ((0, 0), (3, 3), (0, 0)))
    cols = jnp.stack(
        [ordered[:, offset : offset + seq_len, :] for offset in range(7)], axis=0
    ).reshape(7, posts * seq_len, 512)

    vmem = pl.BlockSpec(memory_space=pltpu.VMEM)
    smem = pl.BlockSpec(memory_space=pltpu.SMEM)
    dma = pltpu.SemaphoreType.DMA
    conv_grad, small, pred = pl.pallas_call(
        kernel,
        out_shape=(
            jax.ShapeDtypeStruct((2, 16, 256), F32),
            jax.ShapeDtypeStruct((8, 256), F32),
            jax.ShapeDtypeStruct((8, 128), F32),
        ),
        in_specs=[smem] * 3 + [vmem] * 5,
        out_specs=(vmem, vmem, vmem),
        scratch_shapes=[
            pltpu.VMEM((4, 8, 128), F32),
            pltpu.VMEM((2, 512, 384), jnp.bfloat16),
            pltpu.VMEM((2 * HALF_ROWS, 128), F32),
            pltpu.VMEM((2, KEEP, 128), F32),
            pltpu.VMEM((2, KEEP, 128), F32),
            pltpu.VMEM((2, 2, 4, 128, 128), F32),
            pltpu.VMEM((3, 64, 128), F32),
            pltpu.VMEM((3, 512, 128), F32),
            pltpu.VMEM((7, 64, 128), F32),
            pltpu.VMEM((2, 32, 128), F32),
            pltpu.VMEM((4, 8, 256), F32),
            pltpu.VMEM((8, 256), F32),
            pltpu.VMEM((8, 256), F32),
            pltpu.VMEM((NX, 8, 256), F32),
            pltpu.VMEM((NY, 8, 256), F32),
            dma((3,)), dma((3,)), dma((2,)), dma((2,)), dma((2, 2, 4)), dma((2, 2, 4)),
            dma((3,)), dma((3,)), dma((3,)), dma((3,)), dma((7,)), dma((7,)), dma((2,)), dma((2,)),
            dma((2,)), dma((2,)), dma((3,)), dma((3,)), dma((7,)), dma((7,)),
        ],
        compiler_params=pltpu.CompilerParams(
            collective_id=0, has_side_effects=True, vmem_limit_bytes=40 * 1024 * 1024
        ),
    )(
        occupation, cohort, education,
        jnp.stack([rows8(partial_pred), rows8(offsets), rows8(wage)]),
        jnp.pad(feature, ((0, 0), (0, 5), (0, 0))),
        head_weight,
        cols,
        jnp.stack(shares),
    )
    return (
        conv_grad[:, :15, :],
        small[:3],
        small[4:].reshape(1024)[:840],
        small[3, :40],
        small[3, 128:136],
        pred[:2, 0],
    )


def solution(mesh):
    return jax.shard_map(
        local,
        mesh=mesh,
        in_specs=(
            P("doc", None, None),
            P("doc"),
            P(None, None, "filt"),
            P(None, "filt"),
            P("doc"),
            P("doc"),
            P("doc"),
            P(),
            P(),
            P(),
            P("doc"),
        ),
        out_specs=(P("doc", None, "filt"), P(None, "filt"), P(), P(), P(), P("doc")),
        check_vma=False,
    )
```

```python
import jax
import jax.numpy as jnp
from jax import lax
from jax.experimental import pallas as pl
from jax.experimental.pallas import tpu as pltpu
from jax.sharding import PartitionSpec as P

TAU = 0.05
WIDTH_LIST = ((3, 0), (5, 3), (7, 8))
NZ, NY, NX = 2, 8, 4
HALF_ROWS = 4096
KEEP = 2048
F32 = jnp.float32


def convolve(columns, weights):
    outputs = []
    for taps, first in WIDTH_LIST:
        half = (taps - 1) // 2
        window = columns[:, :, 3 - half : 3 + half + 1, :]
        outputs.append(
            jnp.einsum(
                "ptje,ejf->ptf",
                window,
                weights[:, first : first + taps, :],
                preferred_element_type=jnp.float32,
            )
        )
    return tuple(outputs)


def kernel(
    occ_ref, coh_ref, edu_ref, rows_ref, feat_ref, head_ref, cols_ref, share_ref,
    conv_out, small_out, pred_out,
    pred_buf, slope, grad, from_core, kept, from_y, from_xa, from_xb, from_yb, from_za, from_zb,
    sums, sum_core, sum_z, sum_x, sum_y,
    pred_send, pred_recv, core_send, core_recv, chain_send, chain_recv,
    xa_send, xa_recv, xb_send, xb_recv, yb_send, yb_recv, z_send, z_recv,
    s_send, s_recv, sx_send, sx_recv, sy_send, sy_recv,
):
    doc = lax.axis_index("doc")
    filt = lax.axis_index("filt")
    c = lax.rem(doc, 2)
    x = lax.rem(doc // 2, NX)
    y = lax.rem(doc // (2 * NX), NY)
    z = doc // (2 * NX * NY)

    def at(z_to, y_to, x_to, c_to):
        return {"doc": ((z_to * NY + y_to) * NX + x_to) * 2 + c_to}

    def x_plus(d):
        return lax.rem(x + d, NX)

    def y_plus(d):
        return lax.rem(y + d, NY)

    core_to = at(z, y, x, 1 - c)
    z_to = at(1 - z, y, x, c)
    x_to = [at(z, y, x_plus(d), c) for d in range(1, NX)]
    y_to = [at(z, y_plus(d), x, c) for d in range(1, NY)]
    filt_to = [{"filt": lax.rem(filt + d, 4)} for d in range(1, 4)]

    barrier = pltpu.get_barrier_semaphore()
    partners = [core_to, z_to] + x_to + y_to + filt_to
    for to in partners:
        pl.semaphore_signal(barrier, inc=1, device_id=to, device_id_type=pl.DeviceIdType.MESH)
    pl.semaphore_wait(barrier, len(partners))

    started = []

    def send(src, dst, send_sem, recv_sem, to):
        copy = pltpu.make_async_remote_copy(
            src_ref=src, dst_ref=dst, send_sem=send_sem, recv_sem=recv_sem,
            device_id=to, device_id_type=pl.DeviceIdType.MESH,
        )
        copy.start()
        started.append(copy)
        return copy

    pred_copies = [
        send(rows_ref.at[0], pred_buf.at[filt], pred_send.at[d], pred_recv.at[d], filt_to[d])
        for d in range(3)
    ]
    pred_buf[filt] = rows_ref[0]
    for copy in pred_copies:
        copy.wait_recv()
    pred = pred_buf[0] + pred_buf[1] + pred_buf[2] + pred_buf[3] + rows_ref[1]
    pred_out[...] = pred
    resid = pred - rows_ref[2]

    grid_row = lax.broadcasted_iota(jnp.int32, (8, 256), 0)
    grid_lane = lax.broadcasted_iota(jnp.int32, (8, 256), 1)
    small = jnp.zeros((8, 256), F32)
    for p in range(2):
        r = resid[p : p + 1, :]
        r = jnp.concatenate([r, r], axis=1)
        for w in range(3):
            scale = r * head_ref[w : w + 1, :].astype(F32)
            value = (scale * share_ref[w, p]).astype(jnp.bfloat16)
            for h in range(2):
                slope[h, p * 256 : (p + 1) * 256, w * 128 : (w + 1) * 128] = value[
                    :, h * 128 : (h + 1) * 128
                ]
        rb = jnp.broadcast_to(r, (8, 256))
        zero = jnp.zeros((8, 256), F32)
        small += rb * feat_ref[p]
        small += jnp.where((grid_row - 4) * 256 + grid_lane == occ_ref[p], rb, zero)
        small += jnp.where((grid_row == 3) & (grid_lane == coh_ref[p]), rb, zero)
        small += jnp.where((grid_row == 3) & (grid_lane - 128 == edu_ref[p]), rb, zero)
    sums[0] = small
    s_core = send(sums.at[0], sum_core, s_send.at[0], s_recv.at[0], core_to)

    core_copies = []
    for h in range(2):
        base = h * HALF_ROWS
        for k in range(7):
            low = max(0, abs(k - 3) - 1)
            part = lax.dot_general(
                cols_ref[k, :, h * 256 : (h + 1) * 256],
                slope[h, :, low * 128 :],
                (((0,), (0,)), ((), ())),
                preferred_element_type=F32,
            )
            for w in range(low, 3):
                taps, first = WIDTH_LIST[w]
                tap = first + k - 3 + (taps - 1) // 2
                grad[pl.ds(base + tap, 256, stride=16), :] = part[
                    :, (w - low) * 128 : (w - low + 1) * 128
                ]
        grad[pl.ds(base + 15, 256, stride=16), :] = jnp.zeros((256, 128), F32)
        core_copies.append(
            send(
                grad.at[pl.ds(base + (1 - c) * KEEP, KEEP)],
                from_core.at[h], core_send.at[h], core_recv.at[h], core_to,
            )
        )

    def take_core(h):
        core_copies[h].wait_recv()

        @pl.loop(0, KEEP // 256)
        def _(b):
            rows = pl.ds(b * 256, 256)
            mine = pl.ds(h * HALF_ROWS + c * KEEP + b * 256, 256)
            kept[h, rows, :] = grad[mine, :] + from_core[h, rows, :]

    counts = ((4, 3), (3, 4))
    chain = {}

    def chain_rows(u, owner):
        return pl.ds(owner * 256 + u * 128, 128)

    def chain_step(s):
        for u in range(2):
            for way in range(2):
                n = counts[u][way]
                if s >= n:
                    continue
                owner = y_plus(n - s) if way == 0 else y_plus(NY - n + s)
                rows = chain_rows(u, owner)
                if s > 0:
                    chain[u, way, s - 1].wait_recv()
                    kept[0, rows, :] = kept[0, rows, :] + from_y[u, way, s - 1]
                chain[u, way, s] = send(
                    kept.at[0, rows], from_y.at[u, way, s],
                    chain_send.at[u, way, s], chain_recv.at[u, way, s],
                    y_to[0] if way == 0 else y_to[NY - 2],
                )

    b_counts = ((2, 1), (1, 2))
    b_chain = {}

    def b_rows(u, owner):
        return pl.ds(owner * 512 + u * 256, 256)

    def b_step(s):
        for u in range(2):
            for way in range(2):
                n = b_counts[u][way]
                if s >= n:
                    continue
                owner = x_plus(n - s) if way == 0 else x_plus(NX - n + s)
                rows = b_rows(u, owner)
                if s > 0:
                    b_chain[u, way, s - 1].wait_recv()
                    kept[1, rows, :] = kept[1, rows, :] + from_xb[u, way, s - 1]
                b_chain[u, way, s] = send(
                    kept.at[1, rows], from_xb.at[u, way, s],
                    xb_send.at[u, way, s], xb_recv.at[u, way, s],
                    x_to[0] if way == 0 else x_to[NX - 2],
                )

    take_core(0)
    chain_step(0)
    take_core(1)
    b_step(0)
    s_core.wait_recv()
    sums[1] = sums[0] + sum_core[...]
    s_z = send(sums.at[1], sum_z, s_send.at[1], s_recv.at[1], z_to)
    chain_step(1)
    b_step(1)
    s_z.wait_recv()
    sums[2] = sums[1] + sum_z[...]
    sum_x[x] = sums[2]
    sx = [
        send(sums.at[2], sum_x.at[x], sx_send.at[d - 1], sx_recv.at[d - 1], x_to[d - 1])
        for d in range(1, NX)
    ]
    chain_step(2)
    for copy in sx:
        copy.wait_recv()
    sums[3] = sum_x[0] + sum_x[1] + sum_x[2] + sum_x[3]
    sum_y[y] = sums[3]
    sy = [
        send(sums.at[3], sum_y.at[y], sy_send.at[d - 1], sy_recv.at[d - 1], y_to[d - 1])
        for d in range(1, NY)
    ]
    chain_step(3)

    for u in range(2):
        rows = b_rows(u, x)
        total = kept[1, rows, :]
        for way in range(2):
            last = b_counts[u][way] - 1
            b_chain[u, way, last].wait_recv()
            total += from_xb[u, way, last]
        kept[1, rows, :] = total
    zb = send(
        kept.at[1, pl.ds(x * 512 + (1 - z) * 256, 256)], from_zb, z_send.at[1], z_recv.at[1], z_to
    )

    for u in range(2):
        rows = chain_rows(u, y)
        total = kept[0, rows, :]
        for way in range(2):
            last = counts[u][way] - 1
            chain[u, way, last].wait_recv()
            total += from_y[u, way, last]
        kept[0, rows, :] = total
    xa = [
        send(
            kept.at[0, pl.ds(y * 256 + x_plus(d) * 64, 64)], from_xa.at[d - 1],
            xa_send.at[d - 1], xa_recv.at[d - 1], x_to[d - 1],
        )
        for d in range(1, NX)
    ]

    zb.wait_recv()
    row_b = x * 512 + z * 256
    rows = pl.ds(row_b, 256)
    kept[1, rows, :] = kept[1, rows, :] + from_zb[...]
    yb = [
        send(
            kept.at[1, pl.ds(row_b + y_plus(d) * 32, 32)], from_yb.at[d - 1],
            yb_send.at[d - 1], yb_recv.at[d - 1], y_to[d - 1],
        )
        for d in range(1, NY)
    ]

    for copy in xa:
        copy.wait_recv()
    row_a = y * 256 + x * 64
    rows = pl.ds(row_a, 64)
    kept[0, rows, :] = kept[0, rows, :] + from_xa[0] + from_xa[1] + from_xa[2]
    za = send(kept.at[0, pl.ds(row_a + (1 - z) * 32, 32)], from_za, z_send.at[0], z_recv.at[0], z_to)
    for copy in sy:
        copy.wait_recv()
    total = sum_y[0]
    for d in range(1, NY):
        total += sum_y[d]
    small_out[...] = total
    for copy in yb:
        copy.wait_recv()
    second = kept[1, pl.ds(row_b + y * 32, 32), :]
    for d in range(NY - 1):
        second += from_yb[d]
    za.wait_recv()
    first = kept[0, pl.ds(row_a + z * 32, 32), :] + from_za[...]
    for h, value in enumerate((first, second)):
        for i in range(2):
            conv_out[i, :, h * 128 : (h + 1) * 128] = value[i * 16 : (i + 1) * 16, :]
    for copy in started:
        copy.wait_send()


def place_kernel(conv_ref, small_ref, pred_ref, conv_out, head_out, occ_out, coh_out, edu_out, pred_out):
    for i in range(2):
        conv_out[:, i, :] = conv_ref[i, :15, :]
        pred_out[i] = pred_ref[i, 0]
    head_out[...] = small_ref[:3, :]
    for k in range(4):
        size = min(256, 840 - 256 * k)
        occ_out[256 * k : 256 * k + size] = small_ref[4 + k, :size]
    coh_out[...] = small_ref[3, :40]
    edu_out[...] = small_ref[3, 128:136]


def rows8(values):
    return jnp.pad(jnp.broadcast_to(values[:, None], (2, 128)), ((0, 6), (0, 0)))


def local(
    embedded,
    lengths,
    conv_weight,
    head_weight,
    occupation,
    cohort,
    education,
    occ_table,
    cohort_table,
    edu_table,
    wage,
):
    posts, seq_len, _ = embedded.shape
    positions = jnp.arange(seq_len, dtype=jnp.int32)
    valid = positions[None, :] < lengths[:, None]
    masked = jnp.where(valid[:, :, None], embedded, jnp.zeros_like(embedded))
    padded = jnp.pad(masked, ((0, 0), (3, 3), (0, 0)))
    columns = jnp.stack([padded[:, offset : offset + seq_len, :] for offset in range(7)], axis=2)
    convs = convolve(columns, conv_weight)
    features = []
    shares = []
    for conv in convs:
        score = jnp.where(valid[:, :, None], conv / TAU, -jnp.inf)
        top = jnp.max(score, axis=1, keepdims=True)
        expd = jnp.exp(score - top)
        total = jnp.sum(expd, axis=1, keepdims=True)
        features.append(TAU * (top[:, 0, :] + jnp.log(total[:, 0, :])))
        shares.append(expd / total)
    feature = jnp.stack(features, axis=1)
    head = head_weight.astype(jnp.float32)
    partial_pred = jnp.sum(feature * head[None, :, :], axis=(1, 2))
    occ_hot = (
        occupation[:, None] == jnp.arange(occ_table.shape[0], dtype=jnp.int32)[None, :]
    ).astype(jnp.float32)
    cohort_hot = (
        cohort[:, None] == jnp.arange(cohort_table.shape[0], dtype=jnp.int32)[None, :]
    ).astype(jnp.float32)
    edu_hot = (
        education[:, None] == jnp.arange(edu_table.shape[0], dtype=jnp.int32)[None, :]
    ).astype(jnp.float32)
    offsets = (
        jnp.sum(occ_hot * occ_table[None, :], axis=1)
        + jnp.sum(cohort_hot * cohort_table[None, :], axis=1)
        + jnp.sum(edu_hot * edu_table[None, :], axis=1)
    )

    e = jnp.arange(256, dtype=jnp.int32)[:, None]
    spot = jnp.arange(512, dtype=jnp.int32)[None, :]
    i, c, x, y, z = e % 2, (e // 2) % 2, (e // 4) % 4, (e // 16) % 8, e // 128
    place_a = c * 128 + y * 16 + x * 4 + z * 2 + i
    place_b = 256 + c * 128 + x * 32 + z * 16 + y * 2 + i
    picks = ((spot == place_a) | (spot == place_b)).astype(jnp.bfloat16)
    ordered = jnp.einsum(
        "pte,ek->ptk", masked, picks, preferred_element_type=jnp.float32
    ).astype(jnp.bfloat16)
    ordered = jnp.pad(ordered, ((0, 0), (3, 3), (0, 0)))
    cols = jnp.stack(
        [ordered[:, offset : offset + seq_len, :] for offset in range(7)], axis=0
    ).reshape(7, posts * seq_len, 512)

    vmem = pl.BlockSpec(memory_space=pltpu.VMEM)
    smem = pl.BlockSpec(memory_space=pltpu.SMEM)
    dma = pltpu.SemaphoreType.DMA
    conv_grad, small, pred = pl.pallas_call(
        kernel,
        out_shape=(
            jax.ShapeDtypeStruct((2, 16, 256), F32),
            jax.ShapeDtypeStruct((8, 256), F32),
            jax.ShapeDtypeStruct((8, 128), F32),
        ),
        in_specs=[smem] * 3 + [vmem] * 5,
        out_specs=(vmem, vmem, vmem),
        scratch_shapes=[
            pltpu.VMEM((4, 8, 128), F32),
            pltpu.VMEM((2, 512, 384), jnp.bfloat16),
            pltpu.VMEM((2 * HALF_ROWS, 128), F32),
            pltpu.VMEM((2, KEEP, 128), F32),
            pltpu.VMEM((2, KEEP, 128), F32),
            pltpu.VMEM((2, 2, 4, 128, 128), F32),
            pltpu.VMEM((3, 64, 128), F32),
            pltpu.VMEM((2, 2, 2, 256, 128), F32),
            pltpu.VMEM((7, 32, 128), F32),
            pltpu.VMEM((32, 128), F32),
            pltpu.VMEM((256, 128), F32),
            pltpu.VMEM((4, 8, 256), F32),
            pltpu.VMEM((8, 256), F32),
            pltpu.VMEM((8, 256), F32),
            pltpu.VMEM((NX, 8, 256), F32),
            pltpu.VMEM((NY, 8, 256), F32),
            dma((3,)), dma((3,)), dma((2,)), dma((2,)), dma((2, 2, 4)), dma((2, 2, 4)),
            dma((3,)), dma((3,)), dma((2, 2, 2)), dma((2, 2, 2)), dma((7,)), dma((7,)), dma((2,)), dma((2,)),
            dma((2,)), dma((2,)), dma((3,)), dma((3,)), dma((7,)), dma((7,)),
        ],
        compiler_params=pltpu.CompilerParams(
            collective_id=0, has_side_effects=True, vmem_limit_bytes=40 * 1024 * 1024
        ),
    )(
        occupation, cohort, education,
        jnp.stack([rows8(partial_pred), rows8(offsets), rows8(wage)]),
        jnp.pad(feature, ((0, 0), (0, 5), (0, 0))),
        head_weight,
        cols,
        jnp.stack(shares),
    )
    conv_grad, head_grad, occ_grad, cohort_grad, edu_grad, pred = pl.pallas_call(
        place_kernel,
        out_shape=(
            jax.ShapeDtypeStruct((15, 2, 256), F32),
            jax.ShapeDtypeStruct((3, 256), F32),
            jax.ShapeDtypeStruct((840,), F32),
            jax.ShapeDtypeStruct((40,), F32),
            jax.ShapeDtypeStruct((8,), F32),
            jax.ShapeDtypeStruct((2,), F32),
        ),
        in_specs=[vmem] * 3,
        out_specs=(vmem,) * 5 + (smem,),
        compiler_params=pltpu.CompilerParams(vmem_limit_bytes=2 * 1024 * 1024),
    )(conv_grad, small, pred)
    return (
        jnp.transpose(conv_grad, (1, 0, 2)), head_grad, occ_grad, cohort_grad, edu_grad, pred
    )


def solution(mesh):
    return jax.shard_map(
        local,
        mesh=mesh,
        in_specs=(
            P("doc", None, None),
            P("doc"),
            P(None, None, "filt"),
            P(None, "filt"),
            P("doc"),
            P("doc"),
            P("doc"),
            P(),
            P(),
            P(),
            P("doc"),
        ),
        out_specs=(P("doc", None, "filt"), P(None, "filt"), P(), P(), P(), P("doc")),
        check_vma=False,
    )
```
